256 devices in a mesh: tm: 16 (over z, core), box: 16 (over y, x).
Axes of the slice: x: 4, y: 4, z: 8, core: 2. Of those that a mesh axis runs over, the one named last changes fastest.
Arguments:
- traces: bfloat16 [6, 128, 524288], P(None, 'tm', 'box'), may hold values from -6 to 6
- projection: bfloat16 [16, 256, 128, 128], P('box', 'tm'), may hold values from -0.5 to 0.5
- owner_route: int32 [16, 256, 1], P('box', 'tm'), may hold values from 0 to 15; in each aligned block of 16 rows (0 to 15, 16 to 31, ..., all dimensions but the last counted through in order) at most 2 rows name the same one
- face_slot: int32 [16, 256, 1], P('box', 'tm'), may hold values from 0 to 3
- face_weight: float32 [1024, 128], P(('tm', 'box')), may hold values from 0.2 to 2
Outputs:
- face_load: bfloat16 [1024, 6, 128, 128], P(('tm', 'box'))
The draws below stay inside these ranges and needn't reach their ends.
Inputs may be any that keep to these rules, and one draw needn't show every extreme that they name: `owner_route`: in the aligned blocks of 16 rows (the rows of one device), no owner is named by more than 2 rows, a bound that some block reaches.
All inputs are finite; a program needn't handle non-finite values.
Results may differ from the reference program's by a relative error of at most 0.005.
Values may be sent and summed in bfloat16 or wider, within the bound.
A program may use at most 192 MiB of HBM per device.

```python
import math
import jax
import jax.numpy as jnp
import numpy as np
from jax import lax

COMP = 6
NODES = 128
SAMPLES = 128
BDEV = 16
FCAP = 4
CAP = 2
POINTS = 524288
FACES = 1024
N_TM = 16
N_BOX = 16


def set_ends(result, own_key, low, high):
    spot = [jax.random.randint(jax.random.fold_in(own_key, axis), (), 0, length) for axis, length in enumerate(result.shape)]
    longest = result.shape.index(max(result.shape))
    beside = spot[:longest] + [(spot[longest] + 1) % result.shape[longest]] + spot[longest + 1:]
    return result.at[tuple(spot)].set(low).at[tuple(beside)].set(high)


def shard_levels(key, dims, cuts, smallest, top_value):
    level = 1.0
    for position, blocks in cuts:
        heights = jax.random.uniform(jax.random.fold_in(jax.random.fold_in(key, 6), position), (blocks,), jnp.float32, smallest / len(cuts), top_value / len(cuts))
        level = level * jnp.repeat(jnp.exp(heights), dims[position] // blocks).reshape((-1,) + (1,) * (len(dims) - 1 - position))
    return level


def routed_block(rng, own, number, rows, number_of, top, bound, skew):
    ranking = jax.random.permutation(rng, number_of)
    heavy_load, ordinary = shares(number_of, rows * top, bound, skew, True), shares(number_of, rows * top, bound, skew, False)
    places = jnp.arange(number_of)

    def named(tallies, turn):
        used = int((tallies > 0).sum())
        fixed = max(1, used // 4)
        passed = fixed + (places - fixed + turn * (used - fixed)) % max(1, number_of - fixed)
        return jnp.zeros((number_of,), jnp.int32).at[ranking[jnp.where(places < fixed, places, passed)]].set(jnp.asarray(tallies, jnp.int32))

    tallies = jnp.where(number % 4 == 0, named(heavy_load, number // 4), named(ordinary, number - number // 4 - 1))
    mixed = jax.random.permutation(jax.random.fold_in(own, 3), number_of)
    giver, receiver = mixed[0:number_of // 2 * 2:2], mixed[1:number_of // 2 * 2:2]
    room = jnp.minimum(tallies[giver] - 1, bound - tallies[receiver]) // 2
    room = jnp.where((giver == ranking[0]) | (receiver == ranking[0]) | (tallies[receiver] == 0), 0, jnp.maximum(room, 0))
    passed = jax.random.randint(jax.random.fold_in(own, 4), (number_of // 2,), 0, 1 << 20) % (room + 1)
    tallies = tallies.at[giver].add(-passed).at[receiver].add(passed)
    labels = jnp.searchsorted(jnp.cumsum(tallies), jnp.arange(rows * top), side="right").astype(jnp.int32)
    grid = labels.reshape(top, rows).T
    grid = grid[jax.random.permutation(jax.random.fold_in(own, 1), rows)]
    turn = jax.random.randint(jax.random.fold_in(own, 2), (rows, 1), 0, top)
    return jnp.take_along_axis(grid, (jnp.arange(top)[None, :] + turn) % top, axis=1)


def shares(count, total, limit, lean, full):
    loads = [(1 << 20) // math.isqrt(standing ** lean) + 1 for standing in range(1, count + 1)]
    largest = limit if full else min(limit, max(-(-total // count), total * loads[0] // sum(loads)))
    least = 1 if total - largest >= count - 1 else 0
    holding, spare = [largest] + [least] * (count - 1), total - largest - least * (count - 1)
    while spare > 0:
        candidates = [i for i in range(1, count) if holding[i] < largest] or [i for i in range(1, count) if holding[i] < limit]
        whole, budget = sum([loads[i] for i in candidates]), spare
        for i in candidates:
            addition = min(limit - holding[i], max(1, budget * loads[i] // whole), spare)
            holding[i] = holding[i] + addition
            spare = spare - addition
    return np.array(holding)


def scatter_about(key, dims, deviation, reach, split=(), kind=jnp.bfloat16):
    values = jax.random.normal(key, dims, jnp.float32) * deviation
    if len(split) > 0:
        values = shard_levels(key, dims, split, -0.22, 0.18) * values
    return jnp.clip(values, min=-reach, max=reach).astype(kind)


def setup_inputs(seed: int = 0) -> dict:
    key_of = jax.random.split(jax.random.key(seed), 6)
    traces = scatter_about(key_of[0], (COMP, SAMPLES, POINTS), 1.0, 6.0, ((1, 16), (2, 16)))
    projection = scatter_about(key_of[1], (N_BOX, N_TM * BDEV, NODES, NODES), NODES ** -0.5, 0.5, ((0, 16), (1, 16)))
    owner_route_keys = jax.random.split(jax.random.fold_in(key_of[2], 1), N_BOX * (N_TM * BDEV) // BDEV)
    owner_route_turns = jax.random.permutation(jax.random.fold_in(key_of[2], 3), N_BOX * (N_TM * BDEV) // BDEV)
    owner_route = jax.vmap(lambda own, number: routed_block(jax.random.fold_in(key_of[2], 2), own, number, BDEV, N_BOX, 1, CAP, 2))(owner_route_keys, owner_route_turns).reshape((N_BOX, N_TM * BDEV, 1))
    face_slot = set_ends(jax.random.randint(key_of[3], (N_BOX, N_TM * BDEV, 1), 0, FCAP), jax.random.fold_in(key_of[3], 1), 0, FCAP - 1).astype(jnp.int32)
    face_weight = jnp.clip(jnp.exp(math.log(2.0) - 2.3025851 * jax.random.uniform(key_of[4], (FACES, NODES), jnp.float32) ** shard_levels(key_of[4], (FACES, NODES), ((0, 256),), -0.2, 0.2)), 0.2, 2.0)
    return dict(traces=traces, projection=projection, owner_route=owner_route, face_slot=face_slot, face_weight=face_weight)


def reference(traces, projection, owner_route, face_slot, face_weight):
    series = traces.reshape(COMP, SAMPLES, N_BOX, N_TM, BDEV, NODES)
    matrices = projection.reshape(N_BOX, N_TM, BDEV, NODES, NODES)
    owners = owner_route.reshape(N_BOX, N_TM, BDEV)
    slots = face_slot.reshape(N_BOX, N_TM, BDEV)
    weights = face_weight.reshape(N_TM, N_BOX * FCAP, NODES)

    def one_row(row):
        part = lax.dynamic_index_in_dim(series, row, 3, keepdims=False)
        mats = lax.dynamic_index_in_dim(matrices, row, 1, keepdims=False)
        faces = jnp.einsum("csbjn,bjnm->bjcsm", part.astype(jnp.float32), mats.astype(jnp.float32))
        faces = faces.astype(jnp.bfloat16).astype(jnp.float32)
        row_owner = lax.dynamic_index_in_dim(owners, row, 1, keepdims=False)
        row_slot = lax.dynamic_index_in_dim(slots, row, 1, keepdims=False)
        target = (row_owner * FCAP + row_slot).reshape(-1).astype(jnp.int32)
        summed = jax.ops.segment_sum(faces.reshape(N_BOX * BDEV, COMP, SAMPLES, NODES), target, num_segments=N_BOX * FCAP)
        scale = lax.dynamic_index_in_dim(weights, row, 0, keepdims=False)
        return (summed * scale[:, None, None, :]).astype(jnp.bfloat16)

    rows = lax.map(one_row, jnp.arange(N_TM, dtype=jnp.int32))
    return rows.reshape(FACES, COMP, SAMPLES, NODES)
```

```python
import functools

import jax
import jax.numpy as jnp
from jax import lax
from jax.experimental import pallas as pl
from jax.experimental.pallas import tpu as pltpu
from jax.sharding import PartitionSpec as P

MESH = pl.DeviceIdType.MESH
ZS, CS, YS, XS = 8, 2, 4, 4
BLOCKS = 16
OWNERS = YS * XS
CAP = 2
SLOTS = 4
COMP = 6
ROWS = 8
NODES = 128
HALF = COMP * ROWS
COLS = BLOCKS * NODES
STEPS = ZS


def mod(value, size):
    return lax.rem(value + size, jnp.int32(size))


def offset(step):
    return ((step + 1) // 2) * (2 * lax.rem(step, 2) - 1)


def kernel(
    traces, projection, table, weight, out,
    xbuf, pbuf, fbuf, s1a, s1b, r1a, r1b, s2a, s2b, r2a, r2b, s3, r3,
    tabz, taby, tabx,
    xl_sem, xs_sem, xr_sem, pl_sem, ps_sem, pr_sem, tl_sem, tzs_sem, tzr_sem, txs_sem, txr_sem,
    s1s_sem, s1r_sem, s2s_sem, s2r_sem, s3s_sem, s3r_sem,
):
    tm = lax.axis_index("tm")
    box = lax.axis_index("box")
    z, c = tm // CS, lax.rem(tm, CS)
    y, x = box // XS, lax.rem(box, XS)

    def at(zz, cc, yy, xx):
        return {"tm": zz * CS + cc, "box": yy * XS + xx}

    sibling = at(z, 1 - c, y, x)

    def on_z(dz):
        return at(mod(z + dz, ZS), c, y, x)

    def on_y(dy):
        return at(z, c, mod(y + dy, YS), x)

    def on_x(dx):
        return at(z, c, y, mod(x + dx, XS))

    def remote(src, dst, send, recv, device):
        return pltpu.make_async_remote_copy(
            src_ref=src, dst_ref=dst, send_sem=send, recv_sem=recv, device_id=device, device_id_type=MESH
        )

    def cols(step, core):
        row = mod(z + offset(step), ZS) * CS + core
        return pl.ds(pl.multiple_of(row * COLS, COLS), COLS)

    def x_local(step):
        return pltpu.make_async_copy(traces.at[:, :, cols(step, c)], xbuf.at[step, c], xl_sem.at[step])

    def x_remote(step):
        return remote(
            traces.at[:, :, cols(step, 1 - c)], xbuf.at[step, c], xs_sem.at[step], xr_sem.at[step], sibling
        )

    def x_arrival(step):
        return remote(
            traces.at[:, :, cols(step, 1 - c)], xbuf.at[step, 1 - c], xs_sem.at[step], xr_sem.at[step], sibling
        )

    p_local = pltpu.make_async_copy(projection.at[0], pbuf.at[0], pl_sem.at[0])
    p_local.start()

    def start_local(step, carry):
        x_local(step).start()
        return carry

    lax.fori_loop(0, STEPS, start_local, 0)
    t_local = pltpu.make_async_copy(table, tabz.at[0], tl_sem.at[0])
    t_local.start()

    barrier = pltpu.get_barrier_semaphore()
    pl.semaphore_signal(barrier, inc=1, device_id=sibling, device_id_type=MESH)
    for dz in range(1, ZS):
        pl.semaphore_signal(barrier, inc=1, device_id=on_z(dz), device_id_type=MESH)
    for d in range(1, YS):
        pl.semaphore_signal(barrier, inc=1, device_id=on_y(d), device_id_type=MESH)
        pl.semaphore_signal(barrier, inc=1, device_id=on_x(d), device_id_type=MESH)
    pl.semaphore_wait(barrier, 1 + (ZS - 1) + (YS - 1) + (XS - 1))

    p_first = [
        remote(projection.at[0], pbuf.at[1], ps_sem.at[1], pr_sem.at[1], on_z(-1)),
        remote(projection.at[0], pbuf.at[2], ps_sem.at[2], pr_sem.at[2], on_z(1)),
    ]
    x_remote(0).start()
    for copy in p_first:
        copy.start()

    def table_z(step):
        return remote(table, tabz.at[step], tzs_sem.at[step], tzr_sem.at[step], on_z(-offset(step)))

    def start_remote(step, carry):
        table_z(step).start()
        x_remote(step).start()
        return carry

    lax.fori_loop(1, STEPS, start_remote, 0)

    def forward(step, way):
        return remote(pbuf.at[step], pbuf.at[step + 2], ps_sem.at[step + 2], pr_sem.at[step + 2], on_z(way))

    half_p = BLOCKS // 2
    last_low = remote(
        pbuf.at[5, pl.ds(0, half_p)], pbuf.at[7, pl.ds(0, half_p)], ps_sem.at[7], pr_sem.at[7], on_z(-1)
    )
    last_high = remote(
        pbuf.at[6, pl.ds(half_p, half_p)], pbuf.at[7, pl.ds(half_p, half_p)], ps_sem.at[8], pr_sem.at[8], on_z(1)
    )

    def p_arrival(step):
        return remote(pbuf.at[step], pbuf.at[step], ps_sem.at[step], pr_sem.at[step], on_z(1))

    def stage1(step):
        copies = []
        for d in range(1, YS):
            copies.append(remote(
                s1a.at[step, mod(y + d, YS)], r1a.at[step, d - 1],
                s1s_sem.at[step, d - 1], s1r_sem.at[step, d - 1], on_y(d),
            ))
            copies.append(remote(
                s1b.at[step, mod(x + d, XS)], r1b.at[step, d - 1],
                s1s_sem.at[step, 2 + d], s1r_sem.at[step, 2 + d], on_x(d),
            ))
        return copies

    def stage2(step):
        copies = []
        for d in range(1, YS):
            copies.append(remote(
                s2a.at[step, mod(x + d, XS)], r2a.at[step, d - 1],
                s2s_sem.at[step, d - 1], s2r_sem.at[step, d - 1], on_x(d),
            ))
            copies.append(remote(
                s2b.at[step, mod(y + d, YS)], r2b.at[step, d - 1],
                s2s_sem.at[step, 2 + d], s2r_sem.at[step, 2 + d], on_y(d),
            ))
        return copies

    def stage3(step):
        return remote(s3.at[step], r3.at[step], s3s_sem.at[step], s3r_sem.at[step], on_z(offset(step)))

    def table_xy():
        copies = []
        for d in range(1, YS):
            copies.append(remote(tabz, taby.at[d - 1], txs_sem.at[d - 1], txr_sem.at[d - 1], on_y(d)))
            copies.append(remote(tabz, tabx.at[d - 1], txs_sem.at[2 + d], txr_sem.at[2 + d], on_x(d)))
        return copies

    def produce(step):
        x_local(step).wait()
        x_arrival(step).wait_recv()

        def multiply(j, carry):
            columns = pl.ds(pl.multiple_of(j * NODES, NODES), NODES)
            low = xbuf[step, 0, :, :, columns].reshape(HALF, NODES)
            high = xbuf[step, 1, :, :, columns].reshape(HALF, NODES)
            rows = jnp.concatenate([low, high], axis=0)
            product = jnp.dot(rows, pbuf[step, j], preferred_element_type=jnp.float32)
            fbuf[j] = product.astype(jnp.bfloat16)
            return carry

        lax.fori_loop(0, BLOCKS, multiply, 0)

        def pick(owner, carry):
            oy, ox = owner // XS, lax.rem(owner, XS)
            for rank in range(CAP):
                block = tabz[step, owner * CAP + rank]
                face = fbuf[block]
                s1a[step, oy, ox * CAP + rank] = face[:HALF]
                s1b[step, ox, oy * CAP + rank] = face[HALF:]
            return carry

        lax.fori_loop(0, OWNERS, pick, 0)
        for copy in stage1(step):
            copy.start()

    def merge_first(step, own, theirs, own_table, their_tables, merged, index, here, owner_of):
        def one(lane, carry):
            totals = [jnp.zeros((HALF, NODES), jnp.float32) for _ in range(SLOTS)]
            owner = owner_of(lane)
            for source in range(YS):
                for rank in range(CAP):
                    slot = OWNERS * CAP + owner * CAP + rank
                    if source == 0:
                        tag = own_table[step, slot]
                        value = own[step, here, lane * CAP + rank]
                    else:
                        tag = their_tables[source - 1, step, slot]
                        value = theirs[step, source - 1, lane * CAP + rank]
                    value = value.astype(jnp.float32)
                    for s in range(SLOTS):
                        totals[s] = totals[s] + value * (tag == s).astype(jnp.float32)
            for s in range(SLOTS):
                merged[step, lane, s] = totals[s].astype(jnp.bfloat16)
            return carry

        lax.fori_loop(0, XS, one, 0)

    def merge1(step):
        for copy in stage1(step):
            copy.wait_recv()
        merge_first(step, s1a, r1a, tabz, taby, s2a, 0, y, lambda lane: y * XS + lane)
        merge_first(step, s1b, r1b, tabz, tabx, s2b, 1, x, lambda lane: lane * XS + x)
        for copy in stage2(step):
            copy.start()

    def merge2(step):
        for copy in stage2(step):
            copy.wait_recv()
        for half, (own, theirs, here) in enumerate(((s2a, r2a, x), (s2b, r2b, y))):
            for s in range(SLOTS):
                total = own[step, here, s].astype(jnp.float32)
                for source in range(XS - 1):
                    total = total + theirs[step, source, s].astype(jnp.float32)
                s3[step, s, half] = total.astype(jnp.bfloat16)

        @pl.when(step > 0)
        def _():
            stage3(step).start()

    def advance(i, carry):
        @pl.when(i < STEPS)
        def _():
            @pl.when(i == 0)
            def _():
                p_local.wait()

            @pl.when((lax.rem(i, 2) == 1) & (i < STEPS - 1))
            def _():
                p_arrival(i).wait_recv()
                p_arrival(i + 1).wait_recv()

                @pl.when(i < STEPS - 3)
                def _():
                    forward(i, -1).start()
                    forward(i + 1, 1).start()

                @pl.when(i == STEPS - 3)
                def _():
                    last_low.start()
                    last_high.start()

            @pl.when(i == STEPS - 1)
            def _():
                last_low.wait_recv()
                last_high.wait_recv()

            @pl.when(i == 0)
            def _():
                t_local.wait()

            produce(i)

            @pl.when(i == 0)
            def _():
                def tables(step, carry):
                    table_z(step).wait_recv()
                    return carry

                lax.fori_loop(1, STEPS, tables, 0)
                for copy in table_xy():
                    copy.start()

        @pl.when((i >= 1) & (i < STEPS + 1))
        def _():
            @pl.when(i == 1)
            def _():
                for copy in table_xy():
                    copy.wait_recv()

            merge1(i - 1)

        @pl.when(i >= 2)
        def _():
            merge2(i - 2)

        return carry

    lax.fori_loop(0, STEPS + 2, advance, 0)

    def finish(step, carry):
        source_z = mod(z - offset(step), ZS)

        def place(ref):
            for s in range(SLOTS):
                for half in range(CS):
                    value = ref[step, s, half].astype(jnp.float32) * weight[pl.ds(s, 1), :]
                    value = value.astype(jnp.bfloat16).reshape(COMP, ROWS, NODES)
                    first = pl.multiple_of(source_z * (CS * ROWS) + half * ROWS, ROWS)
                    out[s, :, pl.ds(first, ROWS), :] = value

        @pl.when(step == 0)
        def _():
            place(s3)

        @pl.when(step > 0)
        def _():
            stage3(step).wait_recv()
            place(r3)

        return carry

    lax.fori_loop(0, STEPS, finish, 0)

    x_remote(0).wait_send()
    for copy in p_first:
        copy.wait_send()

    def drain(step, carry):
        table_z(step).wait_send()
        x_remote(step).wait_send()
        stage3(step).wait_send()
        return carry

    lax.fori_loop(1, STEPS, drain, 0)
    for step in (1, 3):
        forward(step, -1).wait_send()
        forward(step + 1, 1).wait_send()
    last_low.wait_send()
    last_high.wait_send()
    for copy in table_xy():
        copy.wait_send()

    def drain_xy(step, carry):
        for copy in stage1(step):
            copy.wait_send()
        for copy in stage2(step):
            copy.wait_send()
        return carry

    lax.fori_loop(0, STEPS, drain_xy, 0)


def fused(traces, projection, table, weight):
    bf16 = jnp.bfloat16
    dma = pltpu.SemaphoreType.DMA
    peers = (YS - 1) + (XS - 1)
    any_space = pl.BlockSpec(memory_space=pl.ANY)
    vmem = pl.BlockSpec(memory_space=pltpu.VMEM)
    return pl.pallas_call(
        kernel,
        out_shape=jax.ShapeDtypeStruct((SLOTS, COMP, ZS * CS * ROWS, NODES), bf16),
        in_specs=[any_space, any_space, pl.BlockSpec(memory_space=pltpu.SMEM), vmem],
        out_specs=vmem,
        scratch_shapes=[
            pltpu.VMEM((STEPS, CS, COMP, ROWS, COLS), bf16),
            pltpu.VMEM((STEPS, BLOCKS, NODES, NODES), bf16),
            pltpu.VMEM((BLOCKS, CS * HALF, NODES), bf16),
            pltpu.VMEM((STEPS, YS, XS * CAP, HALF, NODES), bf16),
            pltpu.VMEM((STEPS, XS, YS * CAP, HALF, NODES), bf16),
            pltpu.VMEM((STEPS, YS - 1, XS * CAP, HALF, NODES), bf16),
            pltpu.VMEM((STEPS, XS - 1, YS * CAP, HALF, NODES), bf16),
            pltpu.VMEM((STEPS, XS, SLOTS, HALF, NODES), bf16),
            pltpu.VMEM((STEPS, YS, SLOTS, HALF, NODES), bf16),
            pltpu.VMEM((STEPS, XS - 1, SLOTS, HALF, NODES), bf16),
            pltpu.VMEM((STEPS, YS - 1, SLOTS, HALF, NODES), bf16),
            pltpu.VMEM((STEPS, SLOTS, CS, HALF, NODES), bf16),
            pltpu.VMEM((STEPS, SLOTS, CS, HALF, NODES), bf16),
            pltpu.SMEM((STEPS, 2 * OWNERS * CAP), jnp.int32),
            pltpu.SMEM((YS - 1, STEPS, 2 * OWNERS * CAP), jnp.int32),
            pltpu.SMEM((XS - 1, STEPS, 2 * OWNERS * CAP), jnp.int32),
            dma((STEPS,)), dma((STEPS,)), dma((STEPS,)),
            dma((1,)), dma((STEPS + 1,)), dma((STEPS + 1,)),
            dma((1,)), dma((STEPS,)), dma((STEPS,)), dma((peers,)), dma((peers,)),
            dma((STEPS, peers)), dma((STEPS, peers)),
            dma((STEPS, peers)), dma((STEPS, peers)),
            dma((STEPS,)), dma((STEPS,)),
        ],
        compiler_params=pltpu.CompilerParams(
            collective_id=0, has_side_effects=True, vmem_limit_bytes=58 * 2**20
        ),
    )(traces, projection, table, weight)


def slot_table(owners, slots):
    same = owners[:, None] == owners[None, :]
    before = jnp.arange(BLOCKS)[None, :] < jnp.arange(BLOCKS)[:, None]
    rank = jnp.sum((same & before).astype(jnp.int32), axis=1)
    place = owners * CAP + rank
    chosen = place[None, :] == jnp.arange(OWNERS * CAP)[:, None]
    block = jnp.sum(jnp.where(chosen, jnp.arange(BLOCKS, dtype=jnp.int32)[None, :], 0), axis=1)
    tag = jnp.sum(jnp.where(chosen, slots[None, :] + 1, 0), axis=1) - 1
    return jnp.concatenate([block, tag]).astype(jnp.int32)


def per_device(traces, projection, owner_route, face_slot, face_weight):
    table = slot_table(owner_route[0, :, 0], face_slot[0, :, 0])
    return fused(traces, projection, table, face_weight)


def solution(mesh):
    return jax.shard_map(
        per_device,
        mesh=mesh,
        in_specs=(
            P(None, "tm", "box"),
            P("box", "tm", None, None),
            P("box", "tm", None),
            P("box", "tm", None),
            P(("tm", "box"), None),
        ),
        out_specs=P(("tm", "box"), None, None, None),
        check_vma=False,
    )
```

```python
import functools

import jax
import jax.numpy as jnp
from jax import lax
from jax.experimental import pallas as pl
from jax.experimental.pallas import tpu as pltpu
from jax.sharding import PartitionSpec as P

MESH = pl.DeviceIdType.MESH
ZS, CS, YS, XS = 8, 2, 4, 4
BLOCKS = 16
OWNERS = YS * XS
CAP = 2
SLOTS = 4
COMP = 6
ROWS = 8
NODES = 128
HALF = COMP * ROWS
COLS = BLOCKS * NODES
STEPS = ZS
FAR = 6
PLUS = (0, 1, 3, 5, FAR)
MINUS = (0, 2, 4, 7, FAR)


def mod(value, size):
    return lax.rem(value + size, jnp.int32(size))


def kernel(
    traces, projection, owners, slots, weight, out,
    xbuf, pbuf, fbuf, s1a, s1b, r1a, r1b, s2a, s2b, r2a, r2b, s3, r3,
    tabz, taby, tabx,
    xl_sem, xs_sem, xr_sem, pl_sem, ps_sem, pr_sem, tzs_sem, tzr_sem, txs_sem, txr_sem,
    s1s_sem, s1r_sem, s2s_sem, s2r_sem, s3s_sem, s3r_sem,
):
    tm = lax.axis_index("tm")
    box = lax.axis_index("box")
    z, c = tm // CS, lax.rem(tm, CS)
    y, x = box // XS, lax.rem(box, XS)
    sign = 1 - 2 * c

    def offset(step):
        place = step + (step // FAR) * (1 - 2 * (step // (FAR + 1)))
        return sign * ((place + 1) // 2) * (2 * lax.rem(place, 2) - 1)

    def at(zz, cc, yy, xx):
        return {"tm": zz * CS + cc, "box": yy * XS + xx}

    sibling = at(z, 1 - c, y, x)

    def on_z(dz):
        return at(mod(z + dz, ZS), c, y, x)

    def on_y(dy):
        return at(z, c, mod(y + dy, YS), x)

    def on_x(dx):
        return at(z, c, y, mod(x + dx, XS))

    def remote(src, dst, send, recv, device):
        return pltpu.make_async_remote_copy(
            src_ref=src, dst_ref=dst, send_sem=send, recv_sem=recv, device_id=device, device_id_type=MESH
        )

    def cols(way, core):
        return pl.ds(pl.multiple_of((mod(z + way, ZS) * CS + core) * COLS, COLS), COLS)

    def x_local(step):
        return pltpu.make_async_copy(traces.at[:, :, cols(offset(step), c)], xbuf.at[step, c], xl_sem.at[step])

    def x_remote(step):
        return remote(
            traces.at[:, :, cols(-offset(step), 1 - c)], xbuf.at[step, c], xs_sem.at[step], xr_sem.at[step], sibling
        )

    def x_arrival(step):
        return remote(
            traces.at[:, :, cols(-offset(step), 1 - c)], xbuf.at[step, 1 - c], xs_sem.at[step], xr_sem.at[step], sibling
        )

    p_local = pltpu.make_async_copy(projection.at[0], pbuf.at[0], pl_sem.at[0])

    def start_local(step, carry):
        x_local(step).start()
        return carry

    x_local(0).start()
    p_local.start()
    lax.fori_loop(1, STEPS, start_local, 0)
    barrier = pltpu.get_barrier_semaphore()
    pl.semaphore_signal(barrier, inc=1, device_id=sibling, device_id_type=MESH)
    for dz in (1, ZS - 1):
        pl.semaphore_signal(barrier, inc=1, device_id=on_z(dz), device_id_type=MESH)
    for d in range(1, YS):
        pl.semaphore_signal(barrier, inc=1, device_id=on_y(d), device_id_type=MESH)
        pl.semaphore_signal(barrier, inc=1, device_id=on_x(d), device_id_type=MESH)

    owner_of_block = [owners[j] for j in range(BLOCKS)]
    code_of_block = [slots[j] + SLOTS * j for j in range(BLOCKS)]

    def own_slots(owner, carry):
        none = jnp.int32(SLOTS * BLOCKS)
        first, last = none, jnp.int32(-1)
        for j in range(BLOCKS):
            match = owner_of_block[j] == owner
            first = jnp.where(match, jnp.minimum(first, code_of_block[j]), first)
            last = jnp.where(match, code_of_block[j], last)
        some, two = first < none, last > first
        first, last = jnp.where(some, first, 0), jnp.where(two, last, 0)
        tabz[0, owner * CAP] = first // SLOTS
        tabz[0, owner * CAP + 1] = last // SLOTS
        tabz[0, OWNERS * CAP + owner * CAP] = jnp.where(some, lax.rem(first, SLOTS), -1)
        tabz[0, OWNERS * CAP + owner * CAP + 1] = jnp.where(two, lax.rem(last, SLOTS), -1)
        return carry

    lax.fori_loop(0, OWNERS, own_slots, 0)
    pl.semaphore_wait(barrier, 1 + 2 + (YS - 1) + (XS - 1))

    half_p = BLOCKS // 2
    low, high = pl.ds(0, half_p), pl.ds(half_p, half_p)

    def ring(hop, turn):
        copies = []
        for way, steps, halves, there in ((0, PLUS, (low, high), -sign), (1, MINUS, (high, low), sign)):
            part = halves[turn]
            src = projection.at[0, part] if hop == 1 else pbuf.at[steps[hop - 1], part]
            copies.append(remote(
                src, pbuf.at[steps[hop], part], ps_sem.at[way, turn, hop - 1], pr_sem.at[way, turn, hop - 1], on_z(there)
            ))
        return copies

    def ring_table(hop):
        copies = []
        for steps, there in ((PLUS, -sign), (MINUS, sign)):
            if hop < 4 or steps is PLUS:
                step = steps[hop]
                copies.append(remote(
                    tabz.at[steps[hop - 1]], tabz.at[step], tzs_sem.at[step], tzr_sem.at[step], on_z(there)
                ))
        return copies

    x_remote(0).start()
    for copy in ring(1, 0) + ring_table(1) + ring(1, 1):
        copy.start()

    def start_remote(step, carry):
        x_remote(step).start()
        return carry

    lax.fori_loop(1, STEPS, start_remote, 0)

    def pass_on(hop, turn):
        arrived = ring(hop, turn) + (ring_table(hop) if turn == 0 else [])
        for copy in arrived:
            copy.wait_recv()
        if hop < 3 or (hop == 3 and turn == 0):
            for copy in ring(hop + 1, turn) + (ring_table(hop + 1) if turn == 0 else []):
                copy.start()

    def stage1(step):
        copies = []
        for d in range(1, YS):
            copies.append(remote(
                s1a.at[step, mod(y + d, YS)], r1a.at[step, d - 1],
                s1s_sem.at[step, d - 1], s1r_sem.at[step, d - 1], on_y(d),
            ))
            copies.append(remote(
                s1b.at[step, mod(x + d, XS)], r1b.at[step, d - 1],
                s1s_sem.at[step, 2 + d], s1r_sem.at[step, 2 + d], on_x(d),
            ))
        return copies

    def stage2(step):
        copies = []
        for d in range(1, YS):
            copies.append(remote(
                s2a.at[step, mod(x + d, XS)], r2a.at[step, d - 1],
                s2s_sem.at[step, d - 1], s2r_sem.at[step, d - 1], on_x(d),
            ))
            copies.append(remote(
                s2b.at[step, mod(y + d, YS)], r2b.at[step, d - 1],
                s2s_sem.at[step, 2 + d], s2r_sem.at[step, 2 + d], on_y(d),
            ))
        return copies

    def stage3(step):
        return remote(s3.at[step], r3.at[step], s3s_sem.at[step], s3r_sem.at[step], on_z(offset(step)))

    def table_xy(step):
        copies = []
        for d in range(1, YS):
            copies.append(remote(
                tabz.at[step], taby.at[step, d - 1], txs_sem.at[step, d - 1], txr_sem.at[step, d - 1], on_y(d)
            ))
            copies.append(remote(
                tabz.at[step], tabx.at[step, d - 1], txs_sem.at[step, 2 + d], txr_sem.at[step, 2 + d], on_x(d)
            ))
        return copies

    def produce(step):
        x_local(step).wait()
        x_arrival(step).wait_recv()

        def multiply(j, carry):
            columns = pl.ds(pl.multiple_of(j * NODES, NODES), NODES)
            low = xbuf[step, 0, :, :, columns].reshape(HALF, NODES)
            high = xbuf[step, 1, :, :, columns].reshape(HALF, NODES)
            rows = jnp.concatenate([low, high], axis=0)
            product = jnp.dot(rows, pbuf[step, j], preferred_element_type=jnp.float32)
            fbuf[j] = product.astype(jnp.bfloat16)
            return carry

        lax.fori_loop(0, BLOCKS, multiply, 0, unroll=4)

        def pick(owner, carry):
            oy, ox = owner // XS, lax.rem(owner, XS)
            for rank in range(CAP):
                block = tabz[step, owner * CAP + rank]
                face = fbuf[block]
                s1a[step, oy, ox * CAP + rank] = face[:HALF]
                s1b[step, ox, oy * CAP + rank] = face[HALF:]
            return carry

        lax.fori_loop(0, OWNERS, pick, 0)
        for copy in table_xy(step) + stage1(step):
            copy.start()

    def merge_first(step, own, theirs, own_table, their_tables, merged, index, here, owner_of):
        def one(lane, carry):
            totals = [jnp.zeros((HALF, NODES), jnp.float32) for _ in range(SLOTS)]
            owner = owner_of(lane)
            for source in range(YS):
                for rank in range(CAP):
                    slot = OWNERS * CAP + owner * CAP + rank
                    if source == 0:
                        tag = own_table[step, slot]
                        value = own[step, here, lane * CAP + rank]
                    else:
                        tag = their_tables[step, source - 1, slot]
                        value = theirs[step, source - 1, lane * CAP + rank]
                    value = value.astype(jnp.float32)
                    for s in range(SLOTS):
                        totals[s] = totals[s] + value * (tag == s).astype(jnp.float32)
            for s in range(SLOTS):
                merged[step, lane, s] = totals[s].astype(jnp.bfloat16)
            return carry

        lax.fori_loop(0, XS, one, 0)

    def merge1(step):
        for copy in table_xy(step) + stage1(step):
            copy.wait_recv()
        merge_first(step, s1a, r1a, tabz, taby, s2a, 0, y, lambda lane: y * XS + lane)
        merge_first(step, s1b, r1b, tabz, tabx, s2b, 1, x, lambda lane: lane * XS + x)
        for copy in stage2(step):
            copy.start()

    def merge2(step):
        for copy in stage2(step):
            copy.wait_recv()
        for half, (own, theirs, here) in enumerate(((s2a, r2a, x), (s2b, r2b, y))):
            for s in range(SLOTS):
                total = own[step, here, s].astype(jnp.float32)
                for source in range(XS - 1):
                    total = total + theirs[step, source, s].astype(jnp.float32)
                s3[step, s, half] = total.astype(jnp.bfloat16)

        @pl.when(step == 2)
        def _():
            stage3(1).start()

        @pl.when(step > 1)
        def _():
            stage3(step).start()

    def advance(i, carry):
        @pl.when(i < STEPS)
        def _():
            @pl.when(i == 0)
            def _():
                p_local.wait()

            @pl.when(i == 1)
            def _():
                merge1(0)

            for hop in range(1, 4):
                @pl.when(i == 2 * hop - 1)
                def _(hop=hop):
                    pass_on(hop, 1)

            @pl.when(i == FAR)
            def _():
                pass_on(4, 0)

            produce(i)

            for hop in range(1, 4):
                @pl.when(i == 2 * hop - 2)
                def _(hop=hop):
                    pass_on(hop, 0)

        @pl.when((i >= 2) & (i < STEPS + 1))
        def _():
            merge1(i - 1)

        @pl.when(i >= 2)
        def _():
            merge2(i - 2)

        return carry

    lax.fori_loop(0, STEPS + 2, advance, 0)

    def finish(step, carry):
        source_z = mod(z - offset(step), ZS)

        def place(ref):
            for s in range(SLOTS):
                for half in range(CS):
                    value = ref[step, s, half].astype(jnp.float32) * weight[pl.ds(s, 1), :]
                    value = value.astype(jnp.bfloat16).reshape(COMP, ROWS, NODES)
                    first = pl.multiple_of(source_z * (CS * ROWS) + half * ROWS, ROWS)
                    out[s, :, pl.ds(first, ROWS), :] = value

        @pl.when(step == 0)
        def _():
            place(s3)

        @pl.when(step > 0)
        def _():
            stage3(step).wait_recv()
            place(r3)

        return carry

    lax.fori_loop(0, STEPS, finish, 0)

    for hop in range(1, 5):
        for copy in ring(hop, 0) + ring_table(hop) + (ring(hop, 1) if hop < 4 else []):
            copy.wait_send()

    def drain(step, carry):
        @pl.when(step > 0)
        def _():
            stage3(step).wait_send()

        x_remote(step).wait_send()
        return carry

    lax.fori_loop(0, STEPS, drain, 0)

    def drain_xy(step, carry):
        for copy in table_xy(step) + stage1(step):
            copy.wait_send()
        for copy in stage2(step):
            copy.wait_send()
        return carry

    lax.fori_loop(0, STEPS, drain_xy, 0)


def fused(traces, projection, owners, slots, weight):
    bf16 = jnp.bfloat16
    dma = pltpu.SemaphoreType.DMA
    peers = (YS - 1) + (XS - 1)
    any_space = pl.BlockSpec(memory_space=pl.ANY)
    vmem = pl.BlockSpec(memory_space=pltpu.VMEM)
    smem = pl.BlockSpec(memory_space=pltpu.SMEM)
    return pl.pallas_call(
        kernel,
        out_shape=jax.ShapeDtypeStruct((SLOTS, COMP, ZS * CS * ROWS, NODES), bf16),
        in_specs=[any_space, any_space, smem, smem, vmem],
        out_specs=vmem,
        scratch_shapes=[
            pltpu.VMEM((STEPS, CS, COMP, ROWS, COLS), bf16),
            pltpu.VMEM((STEPS, BLOCKS, NODES, NODES), bf16),
            pltpu.VMEM((BLOCKS, CS * HALF, NODES), bf16),
            pltpu.VMEM((STEPS, YS, XS * CAP, HALF, NODES), bf16),
            pltpu.VMEM((STEPS, XS, YS * CAP, HALF, NODES), bf16),
            pltpu.VMEM((STEPS, YS - 1, XS * CAP, HALF, NODES), bf16),
            pltpu.VMEM((STEPS, XS - 1, YS * CAP, HALF, NODES), bf16),
            pltpu.VMEM((STEPS, XS, SLOTS, HALF, NODES), bf16),
            pltpu.VMEM((STEPS, YS, SLOTS, HALF, NODES), bf16),
            pltpu.VMEM((STEPS, XS - 1, SLOTS, HALF, NODES), bf16),
            pltpu.VMEM((STEPS, YS - 1, SLOTS, HALF, NODES), bf16),
            pltpu.VMEM((STEPS, SLOTS, CS, HALF, NODES), bf16),
            pltpu.VMEM((STEPS, SLOTS, CS, HALF, NODES), bf16),
            pltpu.SMEM((STEPS, 2 * OWNERS * CAP), jnp.int32),
            pltpu.SMEM((STEPS, YS - 1, 2 * OWNERS * CAP), jnp.int32),
            pltpu.SMEM((STEPS, XS - 1, 2 * OWNERS * CAP), jnp.int32),
            dma((STEPS,)), dma((STEPS,)), dma((STEPS,)),
            dma((1,)), dma((2, 2, 4)), dma((2, 2, 4)),
            dma((STEPS,)), dma((STEPS,)), dma((STEPS, peers)), dma((STEPS, peers)),
            dma((STEPS, peers)), dma((STEPS, peers)),
            dma((STEPS, peers)), dma((STEPS, peers)),
            dma((STEPS,)), dma((STEPS,)),
        ],
        compiler_params=pltpu.CompilerParams(
            collective_id=0, has_side_effects=True, vmem_limit_bytes=58 * 2**20
        ),
    )(traces, projection, owners, slots, weight)


def per_device(traces, projection, owner_route, face_slot, face_weight):
    return fused(traces, projection, owner_route[0, :, 0], face_slot[0, :, 0], face_weight)


def solution(mesh):
    return jax.shard_map(
        per_device,
        mesh=mesh,
        in_specs=(
            P(None, "tm", "box"),
            P("box", "tm", None, None),
            P("box", "tm", None),
            P("box", "tm", None),
            P(("tm", "box"), None),
        ),
        out_specs=P(("tm", "box"), None, None, None),
        check_vma=False,
    )
```

```python
import jax
import jax.numpy as jnp
from jax import lax
from jax.experimental import pallas as pl
from jax.experimental.pallas import tpu as pltpu
from jax.sharding import PartitionSpec as P

MESH = pl.DeviceIdType.MESH
ZS, CS, YS, XS = 8, 2, 4, 4
BLOCKS = 16
OWNERS = YS * XS
CAP = 2
SLOTS = 4
COMP = 6
ROWS = 8
NODES = 128
HALF = COMP * ROWS
COLS = BLOCKS * NODES
STEPS = ZS
FAR = 6
PLUS = (0, 1, 3, 5, FAR)
MINUS = (0, 2, 4, 7, FAR)


def mod(value, size):
    return lax.rem(value + size, jnp.int32(size))


def kernel(
    traces, projection, owners, slots, weight, out,
    xbuf, pbuf, fbuf, s1a, s1b, r1a, r1b, s2a, s2b, r2a, r2b, s3, r3,
    tabz, taby, tabx,
    xl_sem, xs_sem, xr_sem, pl_sem, ps_sem, pr_sem, tzs_sem, tzr_sem, txs_sem, txr_sem,
    s1s_sem, s1r_sem, s2s_sem, s2r_sem, s3s_sem, s3r_sem,
):
    tm = lax.axis_index("tm")
    box = lax.axis_index("box")
    z, c = tm // CS, lax.rem(tm, CS)
    y, x = box // XS, lax.rem(box, XS)
    sign = 1 - 2 * c

    def offset(step):
        place = step + (step // FAR) * (1 - 2 * (step // (FAR + 1)))
        return sign * ((place + 1) // 2) * (2 * lax.rem(place, 2) - 1)

    def at(zz, cc, yy, xx):
        return {"tm": zz * CS + cc, "box": yy * XS + xx}

    sibling = at(z, 1 - c, y, x)

    def on_z(dz):
        return at(mod(z + dz, ZS), c, y, x)

    def on_y(dy):
        return at(z, c, mod(y + dy, YS), x)

    def on_x(dx):
        return at(z, c, y, mod(x + dx, XS))

    def remote(src, dst, send, recv, device):
        return pltpu.make_async_remote_copy(
            src_ref=src, dst_ref=dst, send_sem=send, recv_sem=recv, device_id=device, device_id_type=MESH
        )

    def cols(way, core):
        return pl.ds(pl.multiple_of((mod(z + way, ZS) * CS + core) * COLS, COLS), COLS)

    def x_local(step):
        return pltpu.make_async_copy(traces.at[:, :, cols(offset(step), c)], xbuf.at[step, c], xl_sem.at[step])

    def x_remote(step):
        return remote(
            traces.at[:, :, cols(-offset(step), 1 - c)], xbuf.at[step, c], xs_sem.at[step], xr_sem.at[step], sibling
        )

    def x_arrival(step):
        return remote(
            traces.at[:, :, cols(-offset(step), 1 - c)], xbuf.at[step, 1 - c], xs_sem.at[step], xr_sem.at[step], sibling
        )

    p_local = pltpu.make_async_copy(projection.at[0], pbuf.at[0], pl_sem.at[0])

    def start_local(step, carry):
        x_local(step).start()
        return carry

    x_local(0).start()
    p_local.start()
    lax.fori_loop(1, STEPS, start_local, 0)
    barrier = pltpu.get_barrier_semaphore()
    pl.semaphore_signal(barrier, inc=1, device_id=sibling, device_id_type=MESH)
    for dz in (1, ZS - 1):
        pl.semaphore_signal(barrier, inc=1, device_id=on_z(dz), device_id_type=MESH)
    for d in range(1, YS):
        pl.semaphore_signal(barrier, inc=1, device_id=on_y(d), device_id_type=MESH)
        pl.semaphore_signal(barrier, inc=1, device_id=on_x(d), device_id_type=MESH)

    owner_of_block = [owners[j] for j in range(BLOCKS)]
    code_of_block = [slots[j] + SLOTS * j for j in range(BLOCKS)]

    def own_slots(owner, carry):
        none = jnp.int32(SLOTS * BLOCKS)
        first, last = none, jnp.int32(-1)
        for j in range(BLOCKS):
            match = owner_of_block[j] == owner
            first = jnp.where(match, jnp.minimum(first, code_of_block[j]), first)
            last = jnp.where(match, code_of_block[j], last)
        some, two = first < none, last > first
        first, last = jnp.where(some, first, 0), jnp.where(two, last, 0)
        tabz[0, owner * CAP] = first // SLOTS
        tabz[0, owner * CAP + 1] = last // SLOTS
        tabz[0, OWNERS * CAP + owner * CAP] = jnp.where(some, lax.rem(first, SLOTS), -1)
        tabz[0, OWNERS * CAP + owner * CAP + 1] = jnp.where(two, lax.rem(last, SLOTS), -1)
        return carry

    lax.fori_loop(0, OWNERS, own_slots, 0)
    pl.semaphore_wait(barrier, 1 + 2 + (YS - 1) + (XS - 1))

    half_p = BLOCKS // 2
    low, high = pl.ds(0, half_p), pl.ds(half_p, half_p)

    def ring(hop, turn):
        copies = []
        for way, steps, halves, there in ((0, PLUS, (low, high), -sign), (1, MINUS, (high, low), sign)):
            part = halves[turn]
            src = projection.at[0, part] if hop == 1 else pbuf.at[steps[hop - 1], part]
            copies.append(remote(
                src, pbuf.at[steps[hop], part], ps_sem.at[way, turn, hop - 1], pr_sem.at[way, turn, hop - 1], on_z(there)
            ))
        return copies

    def ring_table(hop):
        copies = []
        for steps, there in ((PLUS, -sign), (MINUS, sign)):
            if hop < 4 or steps is PLUS:
                step = steps[hop]
                copies.append(remote(
                    tabz.at[steps[hop - 1]], tabz.at[step], tzs_sem.at[step], tzr_sem.at[step], on_z(there)
                ))
        return copies

    x_remote(0).start()
    for copy in ring(1, 0) + ring_table(1) + ring(1, 1):
        copy.start()

    def start_remote(step, carry):
        x_remote(step).start()
        return carry

    lax.fori_loop(1, STEPS, start_remote, 0)

    def pass_on(hop, turn):
        arrived = ring(hop, turn) + (ring_table(hop) if turn == 0 else [])
        for copy in arrived:
            copy.wait_recv()
        if hop < 3 or (hop == 3 and turn == 0):
            for copy in ring(hop + 1, turn) + (ring_table(hop + 1) if turn == 0 else []):
                copy.start()

    def stage1(step):
        copies = []
        for d in range(1, YS):
            copies.append(remote(
                s1a.at[step, mod(y + d, YS)], r1a.at[step, d - 1],
                s1s_sem.at[step, d - 1], s1r_sem.at[step, d - 1], on_y(d),
            ))
            copies.append(remote(
                s1b.at[step, mod(x + d, XS)], r1b.at[step, d - 1],
                s1s_sem.at[step, 2 + d], s1r_sem.at[step, 2 + d], on_x(d),
            ))
        return copies

    def stage2(step):
        copies = []
        for d in range(1, YS):
            copies.append(remote(
                s2a.at[step, mod(x + d, XS)], r2a.at[step, d - 1],
                s2s_sem.at[step, d - 1], s2r_sem.at[step, d - 1], on_x(d),
            ))
            copies.append(remote(
                s2b.at[step, mod(y + d, YS)], r2b.at[step, d - 1],
                s2s_sem.at[step, 2 + d], s2r_sem.at[step, 2 + d], on_y(d),
            ))
        return copies

    def stage3(step):
        return remote(s3.at[step], r3.at[step], s3s_sem.at[step], s3r_sem.at[step], on_z(offset(step)))

    def table_xy(step):
        copies = []
        for d in range(1, YS):
            copies.append(remote(
                tabz.at[step], taby.at[step, d - 1], txs_sem.at[step, d - 1], txr_sem.at[step, d - 1], on_y(d)
            ))
            copies.append(remote(
                tabz.at[step], tabx.at[step, d - 1], txs_sem.at[step, 2 + d], txr_sem.at[step, 2 + d], on_x(d)
            ))
        return copies

    def produce(step):
        x_local(step).wait()
        x_arrival(step).wait_recv()

        def multiply(j, carry):
            columns = pl.ds(pl.multiple_of(j * NODES, NODES), NODES)
            low = xbuf[step, 0, :, :, columns].reshape(HALF, NODES)
            high = xbuf[step, 1, :, :, columns].reshape(HALF, NODES)
            rows = jnp.concatenate([low, high], axis=0)
            product = jnp.dot(rows, pbuf[step, j], preferred_element_type=jnp.float32)
            fbuf[j] = product.astype(jnp.bfloat16)
            return carry

        lax.fori_loop(0, BLOCKS, multiply, 0, unroll=16)

        def pick(owner, carry):
            oy, ox = owner // XS, lax.rem(owner, XS)
            for rank in range(CAP):
                block = tabz[step, owner * CAP + rank]
                face = fbuf[block]
                s1a[step, oy, ox * CAP + rank] = face[:HALF]
                s1b[step, ox, oy * CAP + rank] = face[HALF:]
            return carry

        lax.fori_loop(0, OWNERS, pick, 0)
        for copy in table_xy(step) + stage1(step):
            copy.start()

    def merge_first(step, own, theirs, own_table, their_tables, merged, index, here, owner_of):
        def one(lane, carry):
            totals = [jnp.zeros((HALF, NODES), jnp.float32) for _ in range(SLOTS)]
            owner = owner_of(lane)
            for source in range(YS):
                for rank in range(CAP):
                    slot = OWNERS * CAP + owner * CAP + rank
                    if source == 0:
                        tag = own_table[step, slot]
                        value = own[step, here, lane * CAP + rank]
                    else:
                        tag = their_tables[step, source - 1, slot]
                        value = theirs[step, source - 1, lane * CAP + rank]
                    value = value.astype(jnp.float32)
                    for s in range(SLOTS):
                        totals[s] = totals[s] + value * (tag == s).astype(jnp.float32)
            for s in range(SLOTS):
                merged[step, lane, s] = totals[s].astype(jnp.bfloat16)
            return carry

        lax.fori_loop(0, XS, one, 0)

    def merge1(step):
        for copy in table_xy(step) + stage1(step):
            copy.wait_recv()
        merge_first(step, s1a, r1a, tabz, taby, s2a, 0, y, lambda lane: y * XS + lane)
        merge_first(step, s1b, r1b, tabz, tabx, s2b, 1, x, lambda lane: lane * XS + x)
        for copy in stage2(step):
            copy.start()

    def merge2(step):
        for copy in stage2(step):
            copy.wait_recv()
        for half, (own, theirs, here) in enumerate(((s2a, r2a, x), (s2b, r2b, y))):
            for s in range(SLOTS):
                total = own[step, here, s].astype(jnp.float32)
                for source in range(XS - 1):
                    total = total + theirs[step, source, s].astype(jnp.float32)
                s3[step, s, half] = total.astype(jnp.bfloat16)

        @pl.when(step == 2)
        def _():
            stage3(1).start()

        @pl.when(step > 1)
        def _():
            stage3(step).start()

    def advance(i, carry):
        @pl.when(i < STEPS)
        def _():
            @pl.when(i == 0)
            def _():
                p_local.wait()

            @pl.when(i == 1)
            def _():
                merge1(0)

            for hop in range(1, 4):
                @pl.when(i == 2 * hop - 1)
                def _(hop=hop):
                    pass_on(hop, 1)

            @pl.when(i == FAR)
            def _():
                pass_on(4, 0)

            produce(i)

            for hop in range(1, 4):
                @pl.when(i == 2 * hop - 2)
                def _(hop=hop):
                    pass_on(hop, 0)

        @pl.when((i >= 2) & (i < STEPS + 1))
        def _():
            merge1(i - 1)

        @pl.when(i >= 2)
        def _():
            merge2(i - 2)

        return carry

    lax.fori_loop(0, STEPS + 2, advance, 0)

    def finish(step, carry):
        source_z = mod(z - offset(step), ZS)

        def place(ref):
            for s in range(SLOTS):
                for half in range(CS):
                    value = ref[step, s, half].astype(jnp.float32) * weight[pl.ds(s, 1), :]
                    value = value.astype(jnp.bfloat16).reshape(COMP, ROWS, NODES)
                    first = pl.multiple_of(source_z * (CS * ROWS) + half * ROWS, ROWS)
                    out[s, :, pl.ds(first, ROWS), :] = value

        @pl.when(step == 0)
        def _():
            place(s3)

        @pl.when(step > 0)
        def _():
            stage3(step).wait_recv()
            place(r3)

        return carry

    lax.fori_loop(0, STEPS, finish, 0)

    for hop in range(1, 5):
        for copy in ring(hop, 0) + ring_table(hop) + (ring(hop, 1) if hop < 4 else []):
            copy.wait_send()

    def drain(step, carry):
        @pl.when(step > 0)
        def _():
            stage3(step).wait_send()

        x_remote(step).wait_send()
        return carry

    lax.fori_loop(0, STEPS, drain, 0)

    def drain_xy(step, carry):
        for copy in table_xy(step) + stage1(step):
            copy.wait_send()
        for copy in stage2(step):
            copy.wait_send()
        return carry

    lax.fori_loop(0, STEPS, drain_xy, 0)


def fused(traces, projection, owners, slots, weight):
    bf16 = jnp.bfloat16
    dma = pltpu.SemaphoreType.DMA
    peers = (YS - 1) + (XS - 1)
    any_space = pl.BlockSpec(memory_space=pl.ANY)
    vmem = pl.BlockSpec(memory_space=pltpu.VMEM)
    smem = pl.BlockSpec(memory_space=pltpu.SMEM)
    return pl.pallas_call(
        kernel,
        out_shape=pltpu.VMEM((SLOTS, COMP, ZS * CS * ROWS, NODES), bf16),
        in_specs=[any_space, any_space, smem, smem, vmem],
        out_specs=vmem,
        scratch_shapes=[
            pltpu.VMEM((STEPS, CS, COMP, ROWS, COLS), bf16),
            pltpu.VMEM((STEPS, BLOCKS, NODES, NODES), bf16),
            pltpu.VMEM((BLOCKS, CS * HALF, NODES), bf16),
            pltpu.VMEM((STEPS, YS, XS * CAP, HALF, NODES), bf16),
            pltpu.VMEM((STEPS, XS, YS * CAP, HALF, NODES), bf16),
            pltpu.VMEM((STEPS, YS - 1, XS * CAP, HALF, NODES), bf16),
            pltpu.VMEM((STEPS, XS - 1, YS * CAP, HALF, NODES), bf16),
            pltpu.VMEM((STEPS, XS, SLOTS, HALF, NODES), bf16),
            pltpu.VMEM((STEPS, YS, SLOTS, HALF, NODES), bf16),
            pltpu.VMEM((STEPS, XS - 1, SLOTS, HALF, NODES), bf16),
            pltpu.VMEM((STEPS, YS - 1, SLOTS, HALF, NODES), bf16),
            pltpu.VMEM((STEPS, SLOTS, CS, HALF, NODES), bf16),
            pltpu.VMEM((STEPS, SLOTS, CS, HALF, NODES), bf16),
            pltpu.SMEM((STEPS, 2 * OWNERS * CAP), jnp.int32),
            pltpu.SMEM((STEPS, YS - 1, 2 * OWNERS * CAP), jnp.int32),
            pltpu.SMEM((STEPS, XS - 1, 2 * OWNERS * CAP), jnp.int32),
            dma((STEPS,)), dma((STEPS,)), dma((STEPS,)),
            dma((1,)), dma((2, 2, 4)), dma((2, 2, 4)),
            dma((STEPS,)), dma((STEPS,)), dma((STEPS, peers)), dma((STEPS, peers)),
            dma((STEPS, peers)), dma((STEPS, peers)),
            dma((STEPS, peers)), dma((STEPS, peers)),
            dma((STEPS,)), dma((STEPS,)),
        ],
        compiler_params=pltpu.CompilerParams(
            collective_id=0, has_side_effects=True, vmem_limit_bytes=58 * 2**20
        ),
    )(traces, projection, owners, slots, weight)


def per_device(traces, projection, owner_route, face_slot, face_weight):
    return fused(traces, projection, owner_route[0, :, 0], face_slot[0, :, 0], face_weight)


def solution(mesh):
    return jax.shard_map(
        per_device,
        mesh=mesh,
        in_specs=(
            P(None, "tm", "box"),
            P("box", "tm", None, None),
            P("box", "tm", None),
            P("box", "tm", None),
            P(("tm", "box"), None),
        ),
        out_specs=P(("tm", "box"), None, None, None),
        check_vma=False,
    )
```

```python
import jax
import jax.numpy as jnp
from jax import lax
from jax.experimental import pallas as pl
from jax.experimental.pallas import tpu as pltpu
from jax.sharding import PartitionSpec as P

MESH = pl.DeviceIdType.MESH
ZS, CS, YS, XS = 8, 2, 4, 4
BLOCKS = 16
OWNERS = YS * XS
CAP = 2
SLOTS = 4
COMP = 6
ROWS = 8
NODES = 128
HALF = COMP * ROWS
COLS = BLOCKS * NODES
STEPS = ZS
FAR = 6
PLUS = (0, 1, 3, 5, FAR)
MINUS = (0, 2, 4, 7, FAR)


def mod(value, size):
    return lax.rem(value + size, jnp.int32(size))


def kernel(
    traces, projection, owners, slots, weight, out,
    xbuf, pbuf, fbuf, s1a, s1b, r1a, r1b, s2a, s2b, r2a, r2b, s3, r3,
    tabz, taby, tabx,
    xl_sem, xs_sem, xr_sem, pl_sem, ps_sem, pr_sem, tzs_sem, tzr_sem, txs_sem, txr_sem,
    s1s_sem, s1r_sem, s2s_sem, s2r_sem, s3s_sem, s3r_sem,
):
    tm = lax.axis_index("tm")
    box = lax.axis_index("box")
    z, c = tm // CS, lax.rem(tm, CS)
    y, x = box // XS, lax.rem(box, XS)
    sign = 1 - 2 * c

    def offset(step):
        place = step + (step // FAR) * (1 - 2 * (step // (FAR + 1)))
        return sign * ((place + 1) // 2) * (2 * lax.rem(place, 2) - 1)

    def at(zz, cc, yy, xx):
        return {"tm": zz * CS + cc, "box": yy * XS + xx}

    sibling = at(z, 1 - c, y, x)

    def on_z(dz):
        return at(mod(z + dz, ZS), c, y, x)

    def on_y(dy):
        return at(z, c, mod(y + dy, YS), x)

    def on_x(dx):
        return at(z, c, y, mod(x + dx, XS))

    def remote(src, dst, send, recv, device):
        return pltpu.make_async_remote_copy(
            src_ref=src, dst_ref=dst, send_sem=send, recv_sem=recv, device_id=device, device_id_type=MESH
        )

    def cols(way, core):
        return pl.ds(pl.multiple_of((mod(z + way, ZS) * CS + core) * COLS, COLS), COLS)

    def x_local(step):
        return pltpu.make_async_copy(traces.at[:, :, cols(offset(step), c)], xbuf.at[step, c], xl_sem.at[step])

    def x_remote(step):
        return remote(
            traces.at[:, :, cols(-offset(step), 1 - c)], xbuf.at[step, c], xs_sem.at[step], xr_sem.at[step], sibling
        )

    def x_arrival(step):
        return remote(
            traces.at[:, :, cols(-offset(step), 1 - c)], xbuf.at[step, 1 - c], xs_sem.at[step], xr_sem.at[step], sibling
        )

    p_local = pltpu.make_async_copy(projection.at[0], pbuf.at[0], pl_sem.at[0])

    def start_local(step, carry):
        x_local(step).start()
        return carry

    x_local(0).start()
    p_local.start()
    lax.fori_loop(1, STEPS, start_local, 0)
    barrier = pltpu.get_barrier_semaphore()
    pl.semaphore_signal(barrier, inc=1, device_id=sibling, device_id_type=MESH)
    for dz in (1, ZS - 1):
        pl.semaphore_signal(barrier, inc=1, device_id=on_z(dz), device_id_type=MESH)
    for d in range(1, YS):
        pl.semaphore_signal(barrier, inc=1, device_id=on_y(d), device_id_type=MESH)
        pl.semaphore_signal(barrier, inc=1, device_id=on_x(d), device_id_type=MESH)

    owner_of_block = [owners[j] for j in range(BLOCKS)]
    code_of_block = [slots[j] + SLOTS * j for j in range(BLOCKS)]

    def own_slots(owner, carry):
        none = jnp.int32(SLOTS * BLOCKS)
        first, last = none, jnp.int32(-1)
        for j in range(BLOCKS):
            match = owner_of_block[j] == owner
            first = jnp.where(match, jnp.minimum(first, code_of_block[j]), first)
            last = jnp.where(match, code_of_block[j], last)
        some, two = first < none, last > first
        first, last = jnp.where(some, first, 0), jnp.where(two, last, 0)
        tabz[0, owner * CAP] = first // SLOTS
        tabz[0, owner * CAP + 1] = last // SLOTS
        tabz[0, OWNERS * CAP + owner * CAP] = jnp.where(some, lax.rem(first, SLOTS), -1)
        tabz[0, OWNERS * CAP + owner * CAP + 1] = jnp.where(two, lax.rem(last, SLOTS), -1)
        return carry

    lax.fori_loop(0, OWNERS, own_slots, 0)
    pl.semaphore_wait(barrier, 1 + 2 + (YS - 1) + (XS - 1))

    half_p = BLOCKS // 2
    low, high = pl.ds(0, half_p), pl.ds(half_p, half_p)

    def ring(hop, turn):
        copies = []
        for way, steps, halves, there in ((0, PLUS, (low, high), -sign), (1, MINUS, (high, low), sign)):
            part = halves[turn]
            src = projection.at[0, part] if hop == 1 else pbuf.at[steps[hop - 1], part]
            copies.append(remote(
                src, pbuf.at[steps[hop], part], ps_sem.at[way, turn, hop - 1], pr_sem.at[way, turn, hop - 1], on_z(there)
            ))
        return copies

    def ring_table(hop):
        copies = []
        for steps, there in ((PLUS, -sign), (MINUS, sign)):
            if hop < 4 or steps is PLUS:
                step = steps[hop]
                copies.append(remote(
                    tabz.at[steps[hop - 1]], tabz.at[step], tzs_sem.at[step], tzr_sem.at[step], on_z(there)
                ))
        return copies

    x_remote(0).start()
    for copy in ring(1, 0) + ring_table(1) + ring(1, 1):
        copy.start()

    def start_remote(step, carry):
        x_remote(step).start()
        return carry

    lax.fori_loop(1, STEPS, start_remote, 0)

    def pass_on(hop, turn):
        arrived = ring(hop, turn) + (ring_table(hop) if turn == 0 else [])
        for copy in arrived:
            copy.wait_recv()
        if hop < 3 or (hop == 3 and turn == 0):
            for copy in ring(hop + 1, turn) + (ring_table(hop + 1) if turn == 0 else []):
                copy.start()

    def stage1(step):
        copies = []
        for d in range(1, YS):
            copies.append(remote(
                s1a.at[step, mod(y + d, YS)], r1a.at[step, d - 1],
                s1s_sem.at[step, d - 1], s1r_sem.at[step, d - 1], on_y(d),
            ))
            copies.append(remote(
                s1b.at[step, mod(x + d, XS)], r1b.at[step, d - 1],
                s1s_sem.at[step, 2 + d], s1r_sem.at[step, 2 + d], on_x(d),
            ))
        return copies

    def stage2(step):
        copies = []
        for d in range(1, YS):
            copies.append(remote(
                s2a.at[step, mod(x + d, XS)], r2a.at[step, d - 1],
                s2s_sem.at[step, d - 1], s2r_sem.at[step, d - 1], on_x(d),
            ))
            copies.append(remote(
                s2b.at[step, mod(y + d, YS)], r2b.at[step, d - 1],
                s2s_sem.at[step, 2 + d], s2r_sem.at[step, 2 + d], on_y(d),
            ))
        return copies

    def stage3(step):
        return remote(s3.at[step], r3.at[step], s3s_sem.at[step], s3r_sem.at[step], on_z(offset(step)))

    def table_xy(step):
        copies = []
        for d in range(1, YS):
            copies.append(remote(
                tabz.at[step], taby.at[step, d - 1], txs_sem.at[step, d - 1], txr_sem.at[step, d - 1], on_y(d)
            ))
            copies.append(remote(
                tabz.at[step], tabx.at[step, d - 1], txs_sem.at[step, 2 + d], txr_sem.at[step, 2 + d], on_x(d)
            ))
        return copies

    def produce(step):
        x_local(step).wait()
        x_arrival(step).wait_recv()

        def multiply(j, carry):
            columns = pl.ds(pl.multiple_of(j * NODES, NODES), NODES)
            low = xbuf[step, 0, :, :, columns].reshape(HALF, NODES)
            high = xbuf[step, 1, :, :, columns].reshape(HALF, NODES)
            rows = jnp.concatenate([low, high], axis=0)
            product = jnp.dot(rows, pbuf[step, j], preferred_element_type=jnp.float32)
            fbuf[j] = product.astype(jnp.bfloat16)
            return carry

        lax.fori_loop(0, BLOCKS, multiply, 0, unroll=16)

        def pick(owner, carry):
            oy, ox = owner // XS, lax.rem(owner, XS)
            for rank in range(CAP):
                block = tabz[step, owner * CAP + rank]
                face = fbuf[block]
                s1a[step, oy, ox * CAP + rank] = face[:HALF]
                s1b[step, ox, oy * CAP + rank] = face[HALF:]
            return carry

        lax.fori_loop(0, OWNERS, pick, 0, unroll=4)
        for copy in table_xy(step) + stage1(step):
            copy.start()

    def produce_own(core):
        def multiply(j, carry):
            columns = pl.ds(pl.multiple_of(j * NODES, NODES), NODES)
            rows = xbuf[0, core, :, :, columns].reshape(HALF, NODES)
            product = jnp.dot(rows, pbuf[0, j], preferred_element_type=jnp.float32)
            fbuf[j, pl.ds(pl.multiple_of(core * HALF, HALF), HALF)] = product.astype(jnp.bfloat16)
            return carry

        lax.fori_loop(0, BLOCKS, multiply, 0, unroll=16)

        for half in range(CS):
            @pl.when(core == half)
            def _(half=half):
                def pick(owner, carry):
                    oy, ox = owner // XS, lax.rem(owner, XS)
                    for rank in range(CAP):
                        face = fbuf[tabz[0, owner * CAP + rank], half * HALF : (half + 1) * HALF]
                        if half == 0:
                            s1a[0, oy, ox * CAP + rank] = face
                        else:
                            s1b[0, ox, oy * CAP + rank] = face
                    return carry

                lax.fori_loop(0, OWNERS, pick, 0)
                for copy in stage1(0)[half::CS]:
                    copy.start()

    def merge_first(step, own, theirs, own_table, their_tables, merged, index, here, owner_of):
        def one(lane, carry):
            totals = [jnp.zeros((HALF, NODES), jnp.float32) for _ in range(SLOTS)]
            owner = owner_of(lane)
            for source in range(YS):
                for rank in range(CAP):
                    slot = OWNERS * CAP + owner * CAP + rank
                    if source == 0:
                        tag = own_table[step, slot]
                        value = own[step, here, lane * CAP + rank]
                    else:
                        tag = their_tables[step, source - 1, slot]
                        value = theirs[step, source - 1, lane * CAP + rank]
                    value = value.astype(jnp.float32)
                    for s in range(SLOTS):
                        totals[s] = totals[s] + value * (tag == s).astype(jnp.float32)
            for s in range(SLOTS):
                merged[step, lane, s] = totals[s].astype(jnp.bfloat16)
            return carry

        lax.fori_loop(0, XS, one, 0, unroll=2)

    def merge1(step):
        for copy in table_xy(step) + stage1(step):
            copy.wait_recv()
        merge_first(step, s1a, r1a, tabz, taby, s2a, 0, y, lambda lane: y * XS + lane)
        merge_first(step, s1b, r1b, tabz, tabx, s2b, 1, x, lambda lane: lane * XS + x)
        for copy in stage2(step):
            copy.start()

    def merge2(step):
        for copy in stage2(step):
            copy.wait_recv()
        for half, (own, theirs, here) in enumerate(((s2a, r2a, x), (s2b, r2b, y))):
            for s in range(SLOTS):
                total = own[step, here, s].astype(jnp.float32)
                for source in range(XS - 1):
                    total = total + theirs[step, source, s].astype(jnp.float32)
                s3[step, s, half] = total.astype(jnp.bfloat16)

        @pl.when(step > 0)
        def _():
            stage3(step).start()

    def advance(i, carry):
        @pl.when(i < STEPS)
        def _():
            @pl.when(i == 0)
            def _():
                p_local.wait()

            @pl.when(i == 1)
            def _():
                merge1(0)

            for hop in range(1, 4):
                @pl.when(i == 2 * hop - 1)
                def _(hop=hop):
                    pass_on(hop, 1)

            @pl.when(i == FAR)
            def _():
                pass_on(4, 0)

            @pl.when(i == 0)
            def _():
                x_local(0).wait()
                produce_own(c)
                for copy in table_xy(0):
                    copy.start()
                x_arrival(0).wait_recv()
                produce_own(1 - c)

            @pl.when(i > 0)
            def _():
                produce(i)

            for hop in range(1, 4):
                @pl.when(i == 2 * hop - 2)
                def _(hop=hop):
                    pass_on(hop, 0)

        @pl.when((i >= 2) & (i < STEPS + 1))
        def _():
            merge1(i - 1)

        @pl.when(i >= 2)
        def _():
            merge2(i - 2)

        return carry

    lax.fori_loop(0, STEPS + 2, advance, 0)

    def finish(step, carry):
        source_z = mod(z - offset(step), ZS)

        def place(ref):
            for s in range(SLOTS):
                for half in range(CS):
                    value = ref[step, s, half].astype(jnp.float32) * weight[pl.ds(s, 1), :]
                    value = value.astype(jnp.bfloat16).reshape(COMP, ROWS, NODES)
                    first = pl.multiple_of(source_z * (CS * ROWS) + half * ROWS, ROWS)
                    out[s, :, pl.ds(first, ROWS), :] = value

        @pl.when(step == 0)
        def _():
            place(s3)

        @pl.when(step > 0)
        def _():
            stage3(step).wait_recv()
            place(r3)

        return carry

    lax.fori_loop(0, STEPS, finish, 0)

    for hop in range(1, 5):
        for copy in ring(hop, 0) + ring_table(hop) + (ring(hop, 1) if hop < 4 else []):
            copy.wait_send()

    def drain(step, carry):
        @pl.when(step > 0)
        def _():
            stage3(step).wait_send()

        x_remote(step).wait_send()
        return carry

    lax.fori_loop(0, STEPS, drain, 0)

    def drain_xy(step, carry):
        for copy in table_xy(step) + stage1(step):
            copy.wait_send()
        for copy in stage2(step):
            copy.wait_send()
        return carry

    lax.fori_loop(0, STEPS, drain_xy, 0)


def fused(traces, projection, owners, slots, weight):
    bf16 = jnp.bfloat16
    dma = pltpu.SemaphoreType.DMA
    peers = (YS - 1) + (XS - 1)
    any_space = pl.BlockSpec(memory_space=pl.ANY)
    vmem = pl.BlockSpec(memory_space=pltpu.VMEM)
    smem = pl.BlockSpec(memory_space=pltpu.SMEM)
    return pl.pallas_call(
        kernel,
        out_shape=pltpu.VMEM((SLOTS, COMP, ZS * CS * ROWS, NODES), bf16),
        in_specs=[any_space, any_space, smem, smem, vmem],
        out_specs=vmem,
        scratch_shapes=[
            pltpu.VMEM((STEPS, CS, COMP, ROWS, COLS), bf16),
            pltpu.VMEM((STEPS, BLOCKS, NODES, NODES), bf16),
            pltpu.VMEM((BLOCKS, CS * HALF, NODES), bf16),
            pltpu.VMEM((STEPS, YS, XS * CAP, HALF, NODES), bf16),
            pltpu.VMEM((STEPS, XS, YS * CAP, HALF, NODES), bf16),
            pltpu.VMEM((STEPS, YS - 1, XS * CAP, HALF, NODES), bf16),
            pltpu.VMEM((STEPS, XS - 1, YS * CAP, HALF, NODES), bf16),
            pltpu.VMEM((STEPS, XS, SLOTS, HALF, NODES), bf16),
            pltpu.VMEM((STEPS, YS, SLOTS, HALF, NODES), bf16),
            pltpu.VMEM((STEPS, XS - 1, SLOTS, HALF, NODES), bf16),
            pltpu.VMEM((STEPS, YS - 1, SLOTS, HALF, NODES), bf16),
            pltpu.VMEM((STEPS, SLOTS, CS, HALF, NODES), bf16),
            pltpu.VMEM((STEPS, SLOTS, CS, HALF, NODES), bf16),
            pltpu.SMEM((STEPS, 2 * OWNERS * CAP), jnp.int32),
            pltpu.SMEM((STEPS, YS - 1, 2 * OWNERS * CAP), jnp.int32),
            pltpu.SMEM((STEPS, XS - 1, 2 * OWNERS * CAP), jnp.int32),
            dma((STEPS,)), dma((STEPS,)), dma((STEPS,)),
            dma((1,)), dma((2, 2, 4)), dma((2, 2, 4)),
            dma((STEPS,)), dma((STEPS,)), dma((STEPS, peers)), dma((STEPS, peers)),
            dma((STEPS, peers)), dma((STEPS, peers)),
            dma((STEPS, peers)), dma((STEPS, peers)),
            dma((STEPS,)), dma((STEPS,)),
        ],
        compiler_params=pltpu.CompilerParams(
            collective_id=0, has_side_effects=True, vmem_limit_bytes=58 * 2**20
        ),
    )(traces, projection, owners, slots, weight)


def per_device(traces, projection, owner_route, face_slot, face_weight):
    return fused(traces, projection, owner_route[0, :, 0], face_slot[0, :, 0], face_weight)


def solution(mesh):
    return jax.shard_map(
        per_device,
        mesh=mesh,
        in_specs=(
            P(None, "tm", "box"),
            P("box", "tm", None, None),
            P("box", "tm", None),
            P("box", "tm", None),
            P(("tm", "box"), None),
        ),
        out_specs=P(("tm", "box"), None, None, None),
        check_vma=False,
    )
```
